256 devices in a mesh: group: 16 (over y_lo, z), tensor: 16 (over y_hi, x, core).
Axes of the slice: x: 4, y: 4 (y_hi: 2, y_lo: 2; y = y_hi * 2 + y_lo), z: 8, core: 2. Of those that a mesh axis runs over, the one named last changes fastest.
Arguments:
- tokens: bfloat16 [32, 128, 4608], P('group', None, 'tensor'), may hold values from -6 to 6
- targets: bfloat16 [32, 128, 4608], P('group', None, 'tensor'), may hold values from -6 to 6
- token_counts: int32 [32], P('group'), may hold values from 1 to 128, as said below
- sample_counts: int32 [32], replicated, may hold values from 1 to 1000
- up_weight: bfloat16 [6912, 4608], P('tensor'), may hold values from -0.09375 to 0.09375
- down_weight: bfloat16 [6912, 4608], P('tensor'), may hold values from -0.078125 to 0.078125
- momentum_up: float32 [6912, 4608], P('tensor', 'group'), may hold values from -6 to 6
- momentum_down: float32 [6912, 4608], P('tensor', 'group'), may hold values from -6 to 6
Outputs:
- new_momentum_up: float32 [6912, 4608], P('tensor', 'group')
- new_momentum_down: float32 [6912, 4608], P('tensor', 'group')
The draws below stay inside these ranges and needn't reach their ends.
Inputs may be any that keep to these rules, and one draw needn't show every extreme that they name: `token_counts`: some client has exactly 128 valid rows and some exactly 1.
All inputs are finite; a program needn't handle non-finite values.
Results may differ from the reference program's by a relative error of at most 0.02.
Values may be sent and summed in bfloat16 or wider, within the bound.
No kernel may reach another device: no remote copies, remote signals or barrier semaphores. Data moves between devices by JAX's collectives and lax.ppermute only.
A program may use at most 192 MiB of HBM per device.

```python
import jax
import jax.numpy as jnp
from jax import lax

D = 4608
FFW = 6912
ROWS = 128
CL_GRP = 2
STEPS = 2
CLIENTS = 32
N_GROUP = 16
N_TENSOR = 16


def draw_token_counts(key, part):
    counts = jax.random.randint(key, (CLIENTS,), 1, ROWS + 1, dtype=jnp.int32)
    picked = jax.random.permutation(jax.random.fold_in(key, 7), CLIENTS)
    slots_all = jnp.arange(CLIENTS, dtype=jnp.int32)
    counts = jnp.where(slots_all == picked[0], ROWS, counts)
    counts = jnp.where(slots_all == picked[1], 1, counts)
    return counts.astype(jnp.int32)


def plant(array, own_key, smallest, high):
    longest = array.shape.index(max(array.shape))
    spots = []
    for shift in (0, 1):
        where = [jax.random.randint(jax.random.fold_in(own_key, axis), (), 0, length) for axis, length in enumerate(array.shape)]
        where[longest] = (where[longest] + shift) % array.shape[longest]
        spots.append(tuple(where))
    return array.at[spots[0]].set(smallest).at[spots[1]].set(high)


def shard_levels(own_key, extent, shards, low, largest):
    level, own = 1.0, jax.random.fold_in(own_key, 6)
    for position, shards_of in shards:
        draws = jnp.exp(jax.random.uniform(jax.random.fold_in(own, position), (shards_of,), jnp.float32, low / len(shards), largest / len(shards)))
        level = level * jnp.repeat(draws, extent[position] // shards_of).reshape([-1 if axis == position else 1 for axis in range(len(extent))])
    return level


def normal_values(stream_key, extent, spread, most, cuts=(), held_as=jnp.bfloat16):
    array = jax.random.normal(stream_key, extent, jnp.float32) * spread
    if len(cuts) > 0:
        array = shard_levels(stream_key, extent, cuts, -0.22, 0.18) * array
    return jnp.clip(array, min=-most, max=most).astype(held_as)


def setup_inputs(seed: int = 0) -> dict:
    key_of = jax.random.split(jax.random.key(seed), 9)
    tokens = normal_values(key_of[0], (CLIENTS, ROWS, D), 1.0, 6.0, ((0, 16), (2, 16)))
    targets = normal_values(key_of[1], (CLIENTS, ROWS, D), 1.0, 6.0, ((0, 16), (2, 16)))
    token_counts = draw_token_counts(jax.random.fold_in(key_of[8], 71), 0)
    sample_counts = plant(jax.random.randint(key_of[3], (CLIENTS,), 1, 1001), jax.random.fold_in(key_of[3], 1), 1, 1000).astype(jnp.int32)
    up_weight = normal_values(key_of[4], (FFW, D), D ** -0.5, 0.09375, ((0, 16),))
    down_weight = normal_values(key_of[5], (FFW, D), FFW ** -0.5, 0.078125, ((0, 16),))
    momentum_up = normal_values(key_of[6], (FFW, D), 1.0, 6.0, ((0, 16), (1, 16)), jnp.float32)
    momentum_down = normal_values(key_of[7], (FFW, D), 1.0, 6.0, ((0, 16), (1, 16)), jnp.float32)
    return dict(tokens=tokens, targets=targets, token_counts=token_counts, sample_counts=sample_counts, up_weight=up_weight, down_weight=down_weight, momentum_up=momentum_up, momentum_down=momentum_down)


client_rate = 0.0003
momentum_decay = 0.9


def silu_slope(preact):
    logistic = jax.nn.sigmoid(preact)
    return logistic * (1.0 + preact * (1.0 - logistic))


def client_grads(inputs, target, row_mask, weight_up, weight_down):
    preact = lax.dot_general(inputs, weight_up, (((1,), (1,)), ((), ())), preferred_element_type=jnp.float32)
    hidden = jax.nn.silu(preact).astype(jnp.bfloat16)
    blocks = hidden.astype(jnp.float32).reshape(ROWS, N_TENSOR, FFW // N_TENSOR)
    down_blocks = weight_down.astype(jnp.float32).reshape(N_TENSOR, FFW // N_TENSOR, D)
    pieces = jnp.einsum("rkf,kfd->rkd", blocks, down_blocks, precision=lax.Precision.HIGHEST)
    pieces = lax.optimization_barrier(pieces.astype(jnp.bfloat16)).astype(jnp.float32)
    output = jnp.sum(pieces, axis=1)
    residual = (row_mask * (output - target.astype(jnp.float32))).astype(jnp.bfloat16)
    grad_down = lax.dot_general(hidden, residual, (((0,), (0,)), ((), ())), preferred_element_type=jnp.float32)
    back_grad = lax.dot_general(residual, weight_down, (((1,), (1,)), ((), ())), preferred_element_type=jnp.float32)
    slopes = (back_grad * silu_slope(preact)).astype(jnp.bfloat16)
    grad_up = lax.dot_general(slopes, inputs, (((0,), (0,)), ((), ())), preferred_element_type=jnp.float32)
    return grad_up, grad_down


def reference(tokens, targets, token_counts, sample_counts, up_weight, down_weight, momentum_up, momentum_down):
    positions = jnp.arange(ROWS, dtype=jnp.int32)[:, None]

    def group_term(running, group_index):
        acc_up = jnp.zeros((FFW, D), jnp.float32)
        acc_down = jnp.zeros((FFW, D), jnp.float32)
        for slot_num in range(CL_GRP):
            client = (group_index * CL_GRP + slot_num).astype(jnp.int32)
            inputs = lax.dynamic_index_in_dim(tokens, client, 0, keepdims=False)
            target = lax.dynamic_index_in_dim(targets, client, 0, keepdims=False)
            valid_rows = lax.dynamic_index_in_dim(token_counts, client, 0, keepdims=False)
            row_mask = (positions < valid_rows).astype(jnp.float32)
            client_weight = lax.dynamic_index_in_dim(sample_counts, client, 0, keepdims=False).astype(jnp.float32)
            weight_up, weight_down = up_weight, down_weight
            for local_step in range(STEPS):
                grad_up, grad_down = client_grads(inputs, target, row_mask, weight_up, weight_down)
                acc_up = acc_up + client_weight * grad_up
                acc_down = acc_down + client_weight * grad_down
                if local_step + 1 < STEPS:
                    weight_up = (weight_up.astype(jnp.float32) - client_rate * grad_up).astype(jnp.bfloat16)
                    weight_down = (weight_down.astype(jnp.float32) - client_rate * grad_down).astype(jnp.bfloat16)
        group_up = lax.optimization_barrier(acc_up.astype(jnp.bfloat16)).astype(jnp.float32)
        group_down = lax.optimization_barrier(acc_down.astype(jnp.bfloat16)).astype(jnp.float32)
        return (running[0] + group_up, running[1] + group_down), jnp.zeros((), jnp.float32)

    start_sums = (jnp.zeros((FFW, D), jnp.float32), jnp.zeros((FFW, D), jnp.float32))
    (sum_up, sum_down), unused_out = lax.scan(group_term, start_sums, jnp.arange(N_GROUP, dtype=jnp.int32))
    weight_total = jnp.sum(sample_counts).astype(jnp.float32)
    new_momentum_up = momentum_decay * momentum_up + sum_up / weight_total
    new_momentum_down = momentum_decay * momentum_down + sum_down / weight_total
    return (new_momentum_up, new_momentum_down)
```

```python
import functools

import jax
import jax.numpy as jnp
from jax import lax
from jax.experimental import pallas as pl
from jax.experimental.pallas import tpu as pltpu
from jax.sharding import PartitionSpec as P


RATE = 0.0003
DECAY = 0.9
NX, NZ = 4, 8
BF, F32 = jnp.bfloat16, jnp.float32
HBM = pl.BlockSpec(memory_space=pltpu.HBM)
VMEM = pl.BlockSpec(memory_space=pltpu.VMEM)
SMEM = pl.BlockSpec(memory_space=pltpu.SMEM)


def tensor_pairs(source):
    return [
        ((ys * NX + xs) * 2 + cs, (y * NX + x) * 2 + c)
        for y in range(2)
        for x in range(NX)
        for c in range(2)
        for ys, xs, cs in [source(y, x, c)]
    ]


def group_pairs(source):
    return [
        (ls * NZ + zs, l * NZ + z)
        for l in range(2)
        for z in range(NZ)
        for ls, zs in [source(l, z)]
    ]


def from_core(v):
    return lax.ppermute(v, "tensor", tensor_pairs(lambda y, x, c: (y, x, 1 - c)))


def from_y(v):
    return lax.ppermute(v, "tensor", tensor_pairs(lambda y, x, c: (1 - y, x, c)))


def from_x(v, k):
    return lax.ppermute(v, "tensor", tensor_pairs(lambda y, x, c: (y, (x + k) % NX, c)))


def from_z(v, k):
    return lax.ppermute(v, "group", group_pairs(lambda l, z: (l, (z + k) % NZ)))


def from_l(v):
    return lax.ppermute(v, "group", group_pairs(lambda l, z: (1 - l, z)))


def swap_zq(v):
    pairs = [
        (((l * NZ + z) * 2 + y) * 8 + q, ((l * NZ + q) * 2 + y) * 8 + z)
        for l in range(2)
        for z in range(NZ)
        for y in range(2)
        for q in range(8)
    ]
    return lax.ppermute(v, ("group", "tensor"), pairs)


def gather_x(block):
    return [block] + [from_x(block, k) for k in range(1, NX)]


def with_far_core(near):
    return near + [from_core(v) for v in near]


def tie(v, *others):
    return lax.optimization_barrier((v, others))[0]


def fence(*values):
    return lax.optimization_barrier(values)


def in_hbm(values):
    return [pltpu.with_memory_space_constraint(v, pltpu.HBM) for v in values]


def z_near(v):
    return [from_z(v, 1), from_z(v, -1)]


def z_next(got):
    return [from_z(got[0], 1), from_z(got[1], -1)]


def z_order(v, one, two, three, four):
    return [v, one[0], two[0], three[0], four, three[1], two[1], one[1]]


def place_of(i, x, c):
    return lax.rem(x + i % NX, NX) * 2 + (c if i < NX else 1 - c)


def sigmoid(v):
    return 1.0 / (1.0 + jnp.exp(-v))


def silu(v):
    return v / (1.0 + jnp.exp(-v))


def silu_slope(v):
    s = sigmoid(v)
    return s * (1.0 + v * (1.0 - s))


def dot(a, b):
    return jnp.dot(a, b, preferred_element_type=F32)


def dot_nt(a, b):
    return lax.dot_general(a, b, (((1,), (1,)), ((), ())), preferred_element_type=F32)


def dot_tn(a, b):
    return lax.dot_general(a, b, (((0,), (0,)), ((), ())), preferred_element_type=F32)


def same_client(rows):
    half = rows // 2
    first = lax.broadcasted_iota(jnp.int32, (rows, rows), 0) < half
    second = lax.broadcasted_iota(jnp.int32, (rows, rows), 1) < half
    return first == second


SPLIT = 6


def load_chunks(where, chunks, full, sems):
    x, c = where[0], where[1]
    width = chunks[0].shape[1]
    copies = []
    for i, chunk in enumerate(chunks):
        start = pl.multiple_of(place_of(i, x, c) * width, 32)
        copies.append(
            pltpu.make_async_copy(chunk, full.at[:, pl.ds(start, width), :], sems.at[i])
        )
    return copies


def load_weight(weight, held, sems):
    wide = held.shape[1] // SPLIT
    return [
        pltpu.make_async_copy(
            weight.at[:, pl.ds(i * wide, wide)], held.at[:, pl.ds(i * wide, wide)], sems.at[i]
        )
        for i in range(SPLIT)
    ]


def product(weight_copies, chunk_copies, held, full):
    wide = held.shape[1] // SPLIT
    for copy in weight_copies + chunk_copies:
        copy.start()
    for copy in chunk_copies:
        copy.wait()
    total = None
    for i in range(SPLIT):
        weight_copies[i].wait()
        y, at = divmod(i * wide, full.shape[1])
        part = dot(held[:, i * wide : (i + 1) * wide], full[y, at : at + wide, :])
        total = part if total is None else total + part
    return total


def first_kernel(where, weight, *rest):
    chunks, (full, preact, hidden, held, wsem, csem) = rest[:8], rest[8:]
    total = product(load_weight(weight, held, wsem), load_chunks(where, chunks, full, csem), held, full)
    preact[...] = total
    hidden[...] = silu(total).astype(BF)


def second_kernel(where, weight, preact0, hidden0, gram, *rest):
    chunks, (full, slopes0, preact1, hidden1, cross, held, wsem, csem) = rest[:8], rest[8:]
    total = product(load_weight(weight, held, wsem), load_chunks(where, chunks, full, csem), held, full)
    before = preact0[...]
    slopes = (total * silu_slope(before)).astype(BF)
    slopes0[...] = slopes
    after = before - dot(slopes, gram[...])
    preact1[...] = after
    hidden = silu(after).astype(BF)
    hidden1[...] = hidden
    rows = hidden.shape[1]
    overlap = dot_tn(hidden0[...], hidden)
    cross[...] = jnp.where(same_client(rows), -RATE * overlap, 0.0).astype(BF)


def third_kernel(where, weight, residual0, preact1, hidden0, slopes0, weights, *rest):
    chunks, (scaled, held, full, wsem, csem) = rest[:8], rest[8:]
    total = product(load_weight(weight, held, wsem), load_chunks(where, chunks, full, csem), held, full)
    half = full.shape[1]
    rows = full.shape[2]
    overlap = dot(residual0[:, :half], full[0]) + dot(residual0[:, half:], full[1])
    overlap = jnp.where(same_client(rows), RATE * overlap, 0.0).astype(BF)
    total = total - dot(hidden0[...], overlap)
    slopes = (total * silu_slope(preact1[...])).astype(BF).astype(F32)
    scaled[...] = ((slopes + slopes0[...].astype(F32)) * weights[...]).astype(BF)


def params(limit=20 << 20):
    return pltpu.CompilerParams(vmem_limit_bytes=limit)


def cost(flops, size):
    return pl.CostEstimate(flops=flops, bytes_accessed=size, transcendentals=0)


def scratch(units, width, rows):
    return [
        pltpu.VMEM((units, 2 * width * 8), BF),
        pltpu.SemaphoreType.DMA((SPLIT,)),
        pltpu.SemaphoreType.DMA((8,)),
    ]


def first(where, weight, chunks):
    units, rows, width = weight.shape[0], chunks[0].shape[2], chunks[0].shape[1]
    return pl.pallas_call(
        first_kernel,
        out_shape=(
            jax.ShapeDtypeStruct((2, 8 * width, rows), BF),
            jax.ShapeDtypeStruct((units, rows), F32),
            jax.ShapeDtypeStruct((units, rows), BF),
        ),
        in_specs=[SMEM] + [HBM] * 9,
        out_specs=(VMEM,) * 3,
        scratch_shapes=scratch(units, width, rows),
        compiler_params=params(),
        cost_estimate=cost(2 * units * rows * width * 16, 9 << 20),
        name="first",
    )(where, weight, *in_hbm(chunks))


def second(where, weight, preact0, hidden0, gram, chunks):
    units, rows, width = weight.shape[0], chunks[0].shape[2], chunks[0].shape[1]
    return pl.pallas_call(
        second_kernel,
        out_shape=(
            jax.ShapeDtypeStruct((2, 8 * width, rows), BF),
            jax.ShapeDtypeStruct((units, rows), BF),
            jax.ShapeDtypeStruct((units, rows), F32),
            jax.ShapeDtypeStruct((units, rows), BF),
            jax.ShapeDtypeStruct((rows, rows), BF),
        ),
        in_specs=[SMEM, HBM, VMEM, VMEM, VMEM] + [HBM] * 8,
        out_specs=(VMEM,) * 5,
        scratch_shapes=scratch(units, width, rows),
        compiler_params=params(),
        cost_estimate=cost(2 * units * rows * width * 16, 9 << 20),
        name="second",
    )(where, weight, preact0, hidden0, gram, *in_hbm(chunks))


def third(where, weight, residual0, preact1, hidden0, slopes0, weights, chunks):
    units, rows, width = weight.shape[0], chunks[0].shape[2], chunks[0].shape[1]
    held, wsem, csem = scratch(units, width, rows)
    return pl.pallas_call(
        third_kernel,
        out_shape=jax.ShapeDtypeStruct((units, rows), BF),
        in_specs=[SMEM, HBM] + [VMEM] * 5 + [HBM] * 8,
        out_specs=VMEM,
        scratch_shapes=[held, pltpu.VMEM((2, 8 * width, rows), BF), wsem, csem],
        compiler_params=params(),
        cost_estimate=cost(2 * units * rows * width * 16, 9 << 20),
        name="third",
    )(where, weight, residual0, preact1, hidden0, slopes0, weights, *in_hbm(chunks))


def out_kernel(where, weight, hidden, *rest):
    if len(rest) == 1:
        (out,) = rest
        out[0, 0] = dot(weight[...], hidden[...]).astype(BF)
    else:
        residual, cross, out = rest
        total = dot(weight[...], hidden[...]) + dot(residual[0], cross[...])
        out[0, 0] = total.astype(BF)


def half_out(where, flip, weight_t, hidden, extra=()):
    units, rows = hidden.shape
    width = weight_t.shape[0] // 16

    def block(k, y, where):
        x, c = where[0], where[1]
        core = 1 - c if flip else c
        return y, lax.rem(x + k, NX) * 2 + core

    specs = [
        pl.BlockSpec((width, units), lambda k, y, w: (block(k, y, w)[0] * 8 + block(k, y, w)[1], 0)),
        pl.BlockSpec((units, rows), lambda k, y, w: (0, 0)),
    ]
    if extra:
        specs += [
            pl.BlockSpec((1, width, rows), lambda k, y, w: (*block(k, y, w), 0)),
            pl.BlockSpec((rows, rows), lambda k, y, w: (0, 0)),
        ]
    return pl.pallas_call(
        out_kernel,
        out_shape=jax.ShapeDtypeStruct((NX, 2, width, rows), BF),
        grid_spec=pltpu.PrefetchScalarGridSpec(
            num_scalar_prefetch=1,
            grid=(NX, 2),
            in_specs=specs,
            out_specs=pl.BlockSpec((1, 1, width, rows), lambda k, y, w: (k, y, 0, 0)),
        ),
        compiler_params=params(),
        cost_estimate=cost(units * rows * width * 16, 4 << 20),
        name="out_far" if flip else "out_near",
    )(where, weight_t, hidden, *extra)


def final_kernel(picks, where, *rest):
    sets = len(picks)
    lefts = [rest[s * 16 : s * 16 + 8] for s in range(sets)]
    rights = [rest[s * 16 + 8 : s * 16 + 16] for s in range(sets)]
    keep, send, left, right, lsem, rsem = rest[sets * 16 :]
    x, c, l, z = where[0], where[1], where[2], where[3]
    rows = lefts[0][0].shape[1]
    copies = []
    for s in range(sets):
        for i in range(8):
            at_left = pl.multiple_of((s * 8 + lax.rem(z + i, NZ)) * rows, rows)
            at_right = pl.multiple_of((s * 8 + place_of(i, x, c)) * rows, rows)
            source = rights[s][i] if picks[s] is None else rights[s][i].at[picks[s]]
            copies.append(
                pltpu.make_async_copy(lefts[s][i], left.at[:, pl.ds(at_left, rows)], lsem.at[s, i])
            )
            copies.append(
                pltpu.make_async_copy(source, right.at[:, :, pl.ds(at_right, rows)], rsem.at[s, i])
            )
    for copy in copies:
        copy.start()
    for copy in copies:
        copy.wait()
    send[...] = dot_nt(left[...], right[1 - l]).astype(BF)
    keep[...] = dot_nt(left[...], right[l])


def final(where, lefts, rights, picks):
    sets = len(lefts)
    units, rows = lefts[0][0].shape
    width = rights[0][0].shape[-2]
    flat = [v for s in range(sets) for v in list(lefts[s]) + list(rights[s])]
    return pl.pallas_call(
        functools.partial(final_kernel, picks),
        out_shape=(
            jax.ShapeDtypeStruct((units, width), F32),
            jax.ShapeDtypeStruct((units, width), BF),
        ),
        in_specs=[SMEM] + [HBM] * (16 * sets),
        out_specs=(VMEM, VMEM),
        scratch_shapes=[
            pltpu.VMEM((units, sets * 8 * rows), BF),
            pltpu.VMEM((2, width, sets * 8 * rows), BF),
            pltpu.SemaphoreType.DMA((sets, 8)),
            pltpu.SemaphoreType.DMA((sets, 8)),
        ],
        compiler_params=params(),
        cost_estimate=cost(4 * units * rows * width * 8 * sets, 4 << 20),
        name="final",
    )(where, *in_hbm(flat))


def core_sums(where, hidden, weight_t, extra=()):
    far = half_out(where, True, weight_t, hidden, extra)
    got = from_core(far)
    near = half_out(where, False, weight_t, hidden, extra)
    near, got = fence(near, got)
    parts = [near[k].astype(F32) + got[k].astype(F32) for k in range(NX)]
    return parts[0], [v.astype(BF) for v in parts[1:]]


def on_device(
    tokens, targets, token_counts, sample_counts, up_weight, down_weight, momentum_up, momentum_down
):
    slots, length, width = tokens.shape
    rows = slots * length
    tensor, group = lax.axis_index("tensor"), lax.axis_index("group")
    y, x, c = tensor // 8, (tensor // 2) % NX, tensor % 2
    l, z = group // NZ, group % NZ
    where = jnp.stack([x, c, l, z]).astype(jnp.int32)

    def flat(v):
        return v.reshape(rows, width).T

    def both(mine, other):
        return jnp.where(y == 0, jnp.stack([mine, other]), jnp.stack([other, mine]))

    mine = flat(tokens)
    (other,) = fence(from_y(mine))
    token_block = both(mine, other)
    target = tie(flat(targets), other)
    target_other = from_y(target)
    near = gather_x(token_block)
    weight_t = tie(down_weight, other).T

    row = jnp.arange(rows, dtype=jnp.int32)
    count = jnp.where(row < length, token_counts[0], token_counts[1])
    mask = (row % length < count).astype(F32)
    own_counts = lax.dynamic_slice_in_dim(sample_counts, group * slots, slots).astype(F32)
    weights = jnp.where(row < length, own_counts[0], own_counts[1])
    near, target_other, weight_t, mask, weights = fence(
        near, target_other, weight_t, mask, weights
    )
    target_block = both(target, target_other).astype(F32)
    chunks = with_far_core(near)
    chunks, target_block = fence(chunks, target_block)

    full, preact0, hidden0 = first(where, up_weight, chunks)
    own, parts = core_sums(where, hidden0, weight_t)

    def reduced(own, parts):
        return own + sum(v.astype(F32) for v in parts)

    def scattered(parts):
        return [from_x(v, -k) for k, v in enumerate(parts, 1)]

    parts, one = fence(scattered(parts), z_near(hidden0))
    own = reduced(own, parts).astype(BF)
    across, two = fence(from_y(own), z_next(one))
    exact0 = mask * (own.astype(F32) + across.astype(F32) - target_block)
    residual0 = exact0.astype(BF)
    full = full.reshape(2 * 8 * width, rows)
    gram = jnp.where(same_client(rows), RATE * dot_tn(full, full), 0.0).astype(BF)
    near, three = gather_x(residual0), z_next(two)
    pair = jnp.stack([token_block, (exact0 * weights).astype(BF)])
    near, three, gram, pair = fence(near, three, gram, pair)
    chunks, four = fence(with_far_core(near), from_z(three[0], 1))
    hidden0_all = z_order(hidden0, one, two, three, four)

    full0, slopes0, preact1, hidden1, cross = second(
        where, down_weight, preact0, hidden0, gram, chunks
    )

    own, parts = core_sums(
        where, hidden1, weight_t, (full0.reshape(2, 8 * width, rows), cross)
    )
    rows0 = full0.reshape(2 * 8 * width, rows).T
    parts, one, rows0 = fence(scattered(parts), z_near(hidden1), rows0)
    own = reduced(own, parts).astype(BF)
    pair = swap_zq(tie(pair, parts))
    across, two = fence(from_y(own), z_next(one))
    exact1 = mask * (own.astype(F32) + across.astype(F32) - target_block)
    residual1 = exact1.astype(BF)
    last = (exact1 * weights).astype(BF)
    near, three = gather_x(residual1), z_next(two)
    near, three, last, pair = fence(near, three, last, pair)
    last = swap_zq(last)
    chunks, four = fence(with_far_core(near), from_z(three[0], 1))
    hidden1_all = z_order(hidden1, one, two, three, four)
    scaled = third(
        where, down_weight, rows0, preact1, hidden0, slopes0, weights[None, :], chunks
    )

    scaled, pair = fence(scaled, pair)
    one, pair_near = z_near(scaled), gather_x(pair)
    one, last = fence(one, last)
    two = fence(*z_next(one))
    two, pair_near = fence(two, pair_near)
    three, last_near, pair_chunks = z_next(two), gather_x(last), with_far_core(pair_near)
    three, pair_chunks, last_near = fence(three, pair_chunks, last_near)
    four, last_chunks = from_z(three[0], 1), with_far_core(last_near)
    scaled_all = z_order(scaled, one, two, three, four)

    down_keep, down_send = final(
        where, [hidden0_all, hidden1_all], [pair_chunks, last_chunks], (1, None)
    )
    down_got = from_l(down_send)
    up_keep, up_send = final(where, [scaled_all], [pair_chunks], (0,))
    up_got = from_l(tie(up_send, down_got))
    down_sum = down_keep + down_got.astype(F32)
    up_sum = up_keep + up_got.astype(F32)

    weight_total = jnp.sum(sample_counts).astype(F32)
    return (
        DECAY * momentum_up + up_sum / weight_total,
        DECAY * momentum_down + down_sum / weight_total,
    )


def solution(mesh):
    placed = (
        P("group", None, "tensor"),
        P("group", None, "tensor"),
        P("group"),
        P(),
        P("tensor", None),
        P("tensor", None),
        P("tensor", "group"),
        P("tensor", "group"),
    )
    return jax.shard_map(
        on_device,
        mesh=mesh,
        in_specs=placed,
        out_specs=(P("tensor", "group"), P("tensor", "group")),
        check_vma=False,
    )
```
